32 devices in a mesh: group: 4 (over x, core), tensor: 8 (over z, y).
Axes of the slice: x: 2, y: 2, z: 4, core: 2. Of those that a mesh axis runs over, the one named last changes fastest.
Arguments:
- hidden: bfloat16 [512, 8192], P('group'), may hold values from -6 to 6
- norm_gain: bfloat16 [8192], replicated, may hold values from 0.5 to 1.5
- query_matrix: bfloat16 [8192, 8192], P(None, 'tensor'), may hold values from -0.0625 to 0.0625
- output_weight: bfloat16 [8192, 8192], P('tensor'), may hold values from -0.0625 to 0.0625
- kv_pages: bfloat16 [768, 8, 32, 256], P('group', 'tensor'), may hold values from -400 to 400
- page_order: int32 [4, 192], P('group'), may hold values from 0 to 191, each once within a row
- page_counts: int32 [4, 128], P('group'), may hold values from 1 to 8, 192 in all within a row
- page_trims: int32 [4, 128], P('group'), may hold values from 0 to 31
- adapter_store: bfloat16 [32, 8192, 256], P('group', 'tensor'), may hold values from -0.0625 to 0.0625
- store_route: int32 [32, 1], replicated, may hold values from 0 to 3; in each aligned block of 8 rows (0 to 7, 8 to 15, ...) at most 4 rows name the same one
- store_slot: int32 [32], replicated, may hold values from 0 to 7
Outputs:
- layer_out: bfloat16 [512, 8192], P('group')
The draws below stay inside these ranges and needn't reach their ends.
Inputs may be any that keep to these rules, and one draw needn't show every extreme that they name: `store_route`: in each group's block of 8 segments no store group is named more than 4 times. `page_order`: each group's row names each of its 192 pages once. `page_counts`: each group's counts sum to 192.
All inputs are finite; a program needn't handle non-finite values.
Results may differ from the reference program's by a relative error of at most 0.0092.
Values may be sent and summed in bfloat16 or wider, within the bound.
No kernel may reach another device: no remote copies, remote signals or barrier semaphores. Data moves between devices by JAX's collectives and lax.ppermute only.
A program may use at most 128 MiB of HBM per device.

```python
import math
import jax
import jax.numpy as jnp
import numpy as np
from jax import lax

D = 8192
HEADS = 64
KVH = 8
HD = 128
RANK = 64
SEG = 16
HALF = 32
PAGES_MAX = 8
ROWS = 128
ADP_GRP = 8
REQ = 8
CAP = 4
POOL = 192
ADAPTERS = 32
N_GROUP = 4
N_TENSOR = 8


def draw_kv_pages(key, part):
    full_shape = (N_GROUP * POOL, N_TENSOR, HALF, 2 * HD)
    base_key = jax.random.fold_in(key, 11)
    values = jax.random.normal(base_key, full_shape, jnp.float32)
    return jnp.clip(values, -400.0, 400.0).astype(jnp.bfloat16)


def with_ends(values, stream_key, least, largest):
    longest = values.shape.index(max(values.shape))
    spots = []
    for shift in (0, 1):
        where = [jax.random.randint(jax.random.fold_in(stream_key, axis), (), 0, length) for axis, length in enumerate(values.shape)]
        where[longest] = (where[longest] + shift) % values.shape[longest]
        spots.append(tuple(where))
    return values.at[spots[0]].set(least).at[spots[1]].set(largest)


def block_scale(stream_key, shape, cuts, smallest, largest):
    gain, own = 1.0, jax.random.fold_in(stream_key, 6)
    for position, blocks in cuts:
        draws = jnp.exp(jax.random.uniform(jax.random.fold_in(own, position), (blocks,), jnp.float32, smallest / len(cuts), largest / len(cuts)))
        gain = gain * jnp.repeat(draws, shape[position] // blocks).reshape([-1 if axis == position else 1 for axis in range(len(shape))])
    return gain


def profile(amount, total, limit, lean):
    portions = [(1 << 20) // math.isqrt(grade ** lean) + 1 for grade in range(2, amount + 1)]
    surplus, counts = total - limit - (amount - 1), [1] * (amount - 1)
    while surplus > 0:
        movable = [i for i in range(amount - 1) if counts[i] < limit]
        mass, budget = sum([portions[i] for i in movable]), surplus
        for i in movable:
            more = min(limit - counts[i], max(1, budget * portions[i] // mass), surplus)
            counts[i] = counts[i] + more
            surplus = surplus - more
    return np.array([limit] + counts)


def ragged_sizes(key, number_of, total, most, lean):
    if number_of == 2:
        one = jax.random.randint(key, (), max(1, total - most), min(most, total - 1) + 1)
        return jnp.stack([one, total - one])
    tallies = jnp.asarray(profile(number_of, total, most, lean), jnp.int32)
    twos = (number_of - 1) // 2
    source_of, taker = tallies[1:1 + 2 * twos:2], tallies[2:2 + 2 * twos:2]
    room = jnp.minimum(source_of - 1, most - taker)
    shifted = jax.random.randint(jax.random.fold_in(key, 1), (twos,), 0, 1 << 20) % (room + 1)
    tallies = tallies.at[1:1 + 2 * twos:2].set(source_of - shifted).at[2:2 + 2 * twos:2].set(taker + shifted)
    return tallies[jax.random.permutation(jax.random.fold_in(key, 2), number_of)]


def assign_block(stream_key, own, number, rows, amount, top, bound, slope):
    sequence = jax.random.permutation(stream_key, amount)
    heavy_load, ordinary = portions_of(amount, rows * top, bound, slope, True), portions_of(amount, rows * top, bound, slope, False)
    places = jnp.arange(amount)

    def named(sizes, rotation):
        used = int((sizes > 0).sum())
        fixed = max(1, used // 4)
        moved = fixed + (places - fixed + rotation * (used - fixed)) % max(1, amount - fixed)
        return jnp.zeros((amount,), jnp.int32).at[sequence[jnp.where(places < fixed, places, moved)]].set(jnp.asarray(sizes, jnp.int32))

    sizes = jnp.where(number % 4 == 0, named(heavy_load, number // 4), named(ordinary, number - number // 4 - 1))
    mixed = jax.random.permutation(jax.random.fold_in(own, 3), amount)
    giver, sink = mixed[0:amount // 2 * 2:2], mixed[1:amount // 2 * 2:2]
    room = jnp.minimum(sizes[giver] - 1, bound - sizes[sink]) // 2
    room = jnp.where((giver == sequence[0]) | (sink == sequence[0]) | (sizes[sink] == 0), 0, jnp.maximum(room, 0))
    moved = jax.random.randint(jax.random.fold_in(own, 4), (amount // 2,), 0, 1 << 20) % (room + 1)
    sizes = sizes.at[giver].add(-moved).at[sink].add(moved)
    members = jnp.searchsorted(jnp.cumsum(sizes), jnp.arange(rows * top), side="right").astype(jnp.int32)
    listing = members.reshape(top, rows).T
    listing = listing[jax.random.permutation(jax.random.fold_in(own, 1), rows)]
    rotation = jax.random.randint(jax.random.fold_in(own, 2), (rows, 1), 0, top)
    return jnp.take_along_axis(listing, (jnp.arange(top)[None, :] + rotation) % top, axis=1)


def portions_of(number_of, total, most, slope, full):
    portions = [(1 << 20) // math.isqrt(rank ** slope) + 1 for rank in range(1, number_of + 1)]
    largest = most if full else min(most, max(-(-total // number_of), total * portions[0] // sum(portions)))
    least = 1 if total - largest >= number_of - 1 else 0
    given, surplus = [largest] + [least] * (number_of - 1), total - largest - least * (number_of - 1)
    while surplus > 0:
        free = [i for i in range(1, number_of) if given[i] < largest] or [i for i in range(1, number_of) if given[i] < most]
        pool, budget = sum([portions[i] for i in free]), surplus
        for i in free:
            extra = min(most - given[i], max(1, budget * portions[i] // pool), surplus)
            given[i] = given[i] + extra
            surplus = surplus - extra
    return np.array(given)


def normal_values(stream_key, shape, scale, most, cuts=(), held_as=jnp.bfloat16):
    result = jax.random.normal(stream_key, shape, jnp.float32) * scale
    if len(cuts) > 0:
        result = block_scale(stream_key, shape, cuts, -0.22, 0.18) * result
    return jnp.clip(result, min=-most, max=most).astype(held_as)


def setup_inputs(seed: int = 0) -> dict:
    key_list = jax.random.split(jax.random.key(seed), 12)
    hidden = normal_values(key_list[0], (N_GROUP * ROWS, D), 1.0, 6.0, ((0, 4),))
    norm_gain = jnp.clip(1.0 + 0.1 * jax.random.normal(key_list[1], (D,), jnp.float32), 0.5, 1.5).astype(jnp.bfloat16)
    query_matrix = normal_values(key_list[2], (D, D), D ** -0.5, 0.0625, ((1, 8),))
    output_weight = normal_values(key_list[3], (D, D), D ** -0.5, 0.0625, ((0, 8),))
    kv_pages = draw_kv_pages(jax.random.fold_in(key_list[11], 71), 0)
    page_order = jax.vmap(lambda own: jax.random.permutation(own, POOL))(jax.random.split(key_list[5], N_GROUP)).reshape((N_GROUP, POOL)).astype(jnp.int32)
    page_counts = jax.vmap(lambda own: ragged_sizes(own, ROWS, POOL, PAGES_MAX, 2))(jax.random.split(key_list[6], N_GROUP)).reshape((N_GROUP, ROWS)).astype(jnp.int32)
    page_trims = with_ends(jax.random.randint(key_list[7], (N_GROUP, ROWS), 0, HALF), jax.random.fold_in(key_list[7], 1), 0, HALF - 1).astype(jnp.int32)
    adapter_store = normal_values(key_list[8], (ADAPTERS, D, 4 * RANK), D ** -0.5, 0.0625, ((0, 4), (1, 8)))
    store_route_keys = jax.random.split(jax.random.fold_in(key_list[9], 1), (N_GROUP * REQ) // REQ)
    store_route_turns = jax.random.permutation(jax.random.fold_in(key_list[9], 3), (N_GROUP * REQ) // REQ)
    store_route = jax.vmap(lambda own, number: assign_block(jax.random.fold_in(key_list[9], 2), own, number, REQ, N_GROUP, 1, CAP, 2))(store_route_keys, store_route_turns).reshape((N_GROUP * REQ, 1))
    store_slot = with_ends(jax.random.randint(key_list[10], (N_GROUP * REQ,), 0, ADP_GRP), jax.random.fold_in(key_list[10], 1), 0, ADP_GRP - 1).astype(jnp.int32)
    return dict(hidden=hidden, norm_gain=norm_gain, query_matrix=query_matrix, output_weight=output_weight, kv_pages=kv_pages, page_order=page_order, page_counts=page_counts, page_trims=page_trims, adapter_store=adapter_store, store_route=store_route, store_slot=store_slot)


adapter_scale = 2.0
norm_eps = 1e-05
rope_base = 500000.0

def rotate(queries, positions):
    half_dim = queries.shape[-1] // 2
    frequency = rope_base ** (-(jnp.arange(half_dim).astype(jnp.float32) * 2.0) / queries.shape[-1])
    angles = positions[:, None] * frequency[None, :]
    cosine = jnp.cos(angles)[:, None, :]
    sine_table = jnp.sin(angles)[:, None, :]
    lower_part = queries[..., :half_dim]
    upper_part = queries[..., half_dim:]
    return jnp.concatenate([lower_part * cosine - upper_part * sine_table, upper_part * cosine + lower_part * sine_table], axis=-1)

def one_group(group_hidden, group_pages, group_order, group_counts, group_trims, group_route, group_slot, norm_gain, query_matrix, output_weight, adapter_store):
    split_count = N_TENSOR // KVH
    group_heads = HEADS // KVH
    hidden_float32 = group_hidden.astype(jnp.float32)
    inv_rms = lax.rsqrt(lax.optimization_barrier(jnp.mean(hidden_float32 * hidden_float32, axis=1, keepdims=True)) + norm_eps)
    normalized_hidden = (hidden_float32 * inv_rms * norm_gain.astype(jnp.float32)[None, :]).astype(jnp.bfloat16)
    adapter_ids = (group_route * ADP_GRP + group_slot).astype(jnp.int32)
    adapters = adapter_store[adapter_ids].astype(jnp.float32)
    segment_rows = normalized_hidden.astype(jnp.float32).reshape(REQ, SEG, D)
    rank_q = jnp.einsum('ksd,kdr->ksr', segment_rows, adapters[:, :, :RANK]).astype(jnp.bfloat16)
    query_adapter_delta = jnp.einsum('ksr,kdr->ksd', rank_q.astype(jnp.float32), adapters[:, :, 2 * RANK:3 * RANK]).reshape(ROWS, D)
    lengths = (group_counts * split_count * HALF - group_trims).astype(jnp.int32)
    query_float32 = jnp.dot(normalized_hidden, query_matrix, preferred_element_type=jnp.float32) + adapter_scale * query_adapter_delta
    queries = rotate(query_float32.reshape(ROWS, HEADS, HD), (lengths - 1).astype(jnp.float32)).astype(jnp.bfloat16)
    offsets = jnp.cumsum(group_counts) - group_counts
    page_slot = jnp.clip(offsets[:, None] + jnp.arange(PAGES_MAX, dtype=jnp.int32)[None, :], 0, POOL - 1).astype(jnp.int32)
    page_ids = group_order[page_slot]

    def head_block(kv_head):
        head_queries = lax.dynamic_slice_in_dim(queries, kv_head * group_heads, group_heads, 1).astype(jnp.float32)
        maxima = []
        totals = []
        outputs = []
        for part_index in range(split_count):
            column = kv_head * split_count + part_index
            part_cache = lax.dynamic_index_in_dim(group_pages, column, 1, keepdims=False)
            cached = part_cache[page_ids].reshape(ROWS, PAGES_MAX * HALF, 2 * HD).astype(jnp.float32)
            positions = (jnp.arange(PAGES_MAX, dtype=jnp.int32)[:, None] * (split_count * HALF) + part_index * HALF + jnp.arange(HALF, dtype=jnp.int32)[None, :]).reshape(-1)
            usable = positions[None, :] < lengths[:, None]
            scores = jnp.einsum('rgd,rpd->rgp', head_queries, cached[..., :HD]) / math.sqrt(HD)
            masked = jnp.where(usable[:, None, :], scores, -1e+30)
            row_max = lax.optimization_barrier(jnp.max(masked, axis=2))
            weights = jnp.where(usable[:, None, :], jnp.exp(masked - row_max[..., None]), 0.0).astype(jnp.bfloat16)
            totals.append(lax.optimization_barrier(jnp.sum(weights.astype(jnp.float32), axis=2)))
            outputs.append(jnp.einsum('rgp,rpd->rgd', weights.astype(jnp.float32), cached[..., HD:]))
            maxima.append(row_max)
        joint_max = maxima[0]
        for part_index in range(1, split_count):
            joint_max = jnp.maximum(joint_max, maxima[part_index])
        numer = jnp.zeros((ROWS, group_heads, HD), jnp.float32)
        denom = jnp.zeros((ROWS, group_heads), jnp.float32)
        for part_index in range(split_count):
            factor = jnp.exp(maxima[part_index] - joint_max)
            numer = numer + outputs[part_index] * factor[..., None]
            denom = denom + totals[part_index] * factor
        return (numer / denom[..., None]).astype(jnp.bfloat16)
    per_head = lax.map(head_block, jnp.arange(KVH, dtype=jnp.int32))
    attention_result = jnp.moveaxis(per_head, 0, 1).reshape(ROWS, D)
    attended_rows = attention_result.astype(jnp.float32).reshape(REQ, SEG, D)
    rank_o = jnp.einsum('ksd,kdr->ksr', attended_rows, adapters[:, :, RANK:2 * RANK]).astype(jnp.bfloat16)
    output_adapter_delta = jnp.einsum('ksr,kdr->ksd', rank_o.astype(jnp.float32), adapters[:, :, 3 * RANK:]).reshape(ROWS, D)
    projected_rows = jnp.dot(attention_result, output_weight, preferred_element_type=jnp.float32)
    return (hidden_float32 + (projected_rows + adapter_scale * output_adapter_delta)).astype(jnp.bfloat16)

def reference(hidden, norm_gain, query_matrix, output_weight, kv_pages, page_order, page_counts, page_trims, adapter_store, store_route, store_slot):
    stacked = (hidden.reshape(N_GROUP, ROWS, D), kv_pages.reshape(N_GROUP, POOL, N_TENSOR, HALF, 2 * HD), page_order, page_counts, page_trims, store_route.reshape(N_GROUP, REQ), store_slot.reshape(N_GROUP, REQ))

    def per_group(items):
        return one_group(items[0], items[1], items[2], items[3], items[4], items[5], items[6], norm_gain, query_matrix, output_weight, adapter_store)
    layer_out = lax.map(per_group, stacked)
    return layer_out.reshape(N_GROUP * ROWS, D)
```

```python
import functools
import math

import jax
import jax.numpy as jnp
from jax import lax
from jax.experimental import pallas as pl
from jax.experimental.pallas import tpu as pltpu
from jax.sharding import PartitionSpec as P

KVH = 8
HD = 128
SEG = 16
PAGES_MAX = 8
LANES = 128
SLOTS = 8

adapter_scale = 2.0
norm_eps = 1e-05
rope_base = 500000.0
hidden_mask = -1e30

f32 = jnp.float32
bf16 = jnp.bfloat16
VMEM = pl.BlockSpec(memory_space=pltpu.VMEM)
SMEM = pl.BlockSpec(memory_space=pltpu.SMEM)
NT = (((1,), (1,)), ((), ()))
TN = (((0,), (0,)), ((), ()))


def cost(flops, traffic):
    return pl.CostEstimate(flops=int(flops), bytes_accessed=int(traffic), transcendentals=0)


def params():
    return pltpu.CompilerParams(vmem_limit_bytes=48 << 20)


def flip(value, axis, bits):
    return lax.ppermute(value, axis, [(i, i ^ bits) for i in range(lax.axis_size(axis))])


def tables(positions):
    half = HD // 2
    frequency = rope_base ** (-(jnp.arange(half).astype(f32) * 2.0) / HD)
    angles = positions[:, None] * frequency[None, :]
    cosine, sine = jnp.cos(angles), jnp.sin(angles)
    return jnp.concatenate([cosine, cosine], 1), jnp.concatenate([-sine, sine], 1)


def prep_kernel(half_size, counts_ref, trims_ref, owner_ref, mask_ref, row_ref):
    slots, rows = owner_ref.shape
    counts = counts_ref[...].astype(f32)
    trims = trims_ref[...].astype(f32)
    before = lax.broadcasted_iota(jnp.int32, (rows, rows), 0)
    after = lax.broadcasted_iota(jnp.int32, (rows, rows), 1)
    earlier = jnp.where(before < after, 1.0, 0.0).astype(bf16)
    start = jnp.dot(
        jnp.broadcast_to(counts, (8, rows)).astype(bf16), earlier, preferred_element_type=f32
    )[0:1]
    end = start + counts
    slot = lax.broadcasted_iota(jnp.int32, (slots, rows), 0).astype(f32)
    owner = jnp.where((slot >= start) & (slot < end), 1.0, 0.0)
    owner_ref[...] = owner
    last = jnp.where(slot == end - 1.0, trims, 0.0)
    used = half_size - jnp.sum(last, axis=1, keepdims=True)
    row = lax.broadcasted_iota(jnp.int32, (slots, rows), 1).astype(f32)
    row_ref[...] = jnp.broadcast_to(
        jnp.sum(owner * row, axis=1, keepdims=True), row_ref.shape
    )
    shape = mask_ref.shape
    place = lax.broadcasted_iota(jnp.int32, shape, 0) % SLOTS
    column = lax.broadcasted_iota(jnp.int32, shape, 1)
    fits = (column // half_size == place) & ((column % half_size).astype(f32) < used)
    mask_ref[...] = jnp.where(fits, 0.0, hidden_mask)


def prepare(counts, trims, slots, half_size):
    rows = counts.shape[1]
    return pl.pallas_call(
        functools.partial(prep_kernel, half_size),
        out_shape=(
            jax.ShapeDtypeStruct((slots, rows), f32),
            jax.ShapeDtypeStruct((slots, SLOTS * half_size), f32),
            jax.ShapeDtypeStruct((slots, LANES), f32),
        ),
        in_specs=[VMEM, VMEM],
        out_specs=(VMEM, VMEM, VMEM),
        compiler_params=params(),
        cost_estimate=cost(1e6, 5e5),
        name="prep",
    )(counts, trims)


def attention_kernel(
    heads, extra, fused, order_ref, query_ref, inv_ref, *refs
):
    deltas, refs = refs[:extra], refs[extra:]
    cos_ref, sin_ref, owner_ref, mask_ref, row_ref, kv_ref = refs[:6]
    outs = refs[6:-4]
    q_scr, o_scr, m_scr, l_scr = refs[-4:]
    slots = owner_ref.shape[0]
    steps = slots // SLOTS
    half_size = kv_ref.shape[2]
    owner = owner_ref[...]
    owner_low = owner.astype(bf16)
    for head in range(heads):
        lanes = slice(head * HD, (head + 1) * HD)
        value = query_ref[:, lanes]
        if fused:
            for ref in deltas:
                value = value + adapter_scale * ref[0, :, lanes].astype(f32)
            value = value * inv_ref[...]
            value = value * cos_ref[...] + pltpu.roll(value, HD // 2, 1) * sin_ref[...]
        spread = jnp.dot(owner_low, value.astype(bf16), preferred_element_type=f32)
        q_scr[:, head * SLOTS : (head + 1) * SLOTS, :] = spread.reshape(steps, SLOTS, HD)

    def step(b, carry):
        pages = [kv_ref[order_ref[0, b * SLOTS + i], 0] for i in range(SLOTS)]
        keys = jnp.concatenate([page[:, :HD] for page in pages], axis=0)
        values = jnp.concatenate([page[:, HD:] for page in pages], axis=0)
        scores = lax.dot_general(
            q_scr[b].astype(bf16), keys, NT, preferred_element_type=f32
        ) * (1.0 / math.sqrt(HD))
        width = SLOTS * half_size
        mask = mask_ref[pl.ds(pl.multiple_of(b * SLOTS, SLOTS), SLOTS), :]
        scores = (scores.reshape(heads, SLOTS, width) + mask[None]).reshape(heads * SLOTS, width)
        top = jnp.max(scores, axis=1, keepdims=True)
        weights = jnp.exp(scores - top).astype(bf16)
        total = jnp.sum(weights.astype(f32), axis=1, keepdims=True)
        o_scr[b] = jnp.dot(weights, values, preferred_element_type=f32)
        m_scr[b] = jnp.broadcast_to(top, (heads * SLOTS, LANES))
        l_scr[b] = jnp.broadcast_to(total, (heads * SLOTS, LANES))
        return carry

    lax.fori_loop(0, steps, step, 0, unroll=4 if steps % 4 == 0 else 1)

    lane = lax.broadcasted_iota(jnp.int32, (slots, LANES), 1)
    tops = jnp.zeros((slots, LANES), f32)
    totals = jnp.zeros((slots, LANES), f32)
    for head in range(heads):
        part = slice(head * SLOTS, (head + 1) * SLOTS)
        tops = jnp.where(lane == head, m_scr[:, part, :].reshape(slots, LANES), tops)
        totals = jnp.where(lane == head, l_scr[:, part, :].reshape(slots, LANES), totals)
    row = row_ref[...]
    joint = tops
    distance = 1
    while distance < PAGES_MAX:
        for shift in (distance, slots - distance):
            same = pltpu.roll(row, shift, 0) == row
            joint = jnp.where(same, jnp.maximum(joint, pltpu.roll(joint, shift, 0)), joint)
        distance *= 2
    factor = jnp.exp(tops - joint)
    dot = functools.partial(
        lax.dot_general,
        dimension_numbers=TN,
        precision=lax.Precision.HIGHEST,
        preferred_element_type=f32,
    )
    denom = dot(owner, totals * factor)
    for head in range(heads):
        part = slice(head * SLOTS, (head + 1) * SLOTS)
        lanes = slice(head * HD, (head + 1) * HD)
        value = o_scr[:, part, :].reshape(slots, HD) * factor[:, head : head + 1]
        numer = dot(owner, value)
        if fused:
            outs[0][:, lanes] = (numer / denom[:, head : head + 1]).astype(bf16)
        else:
            outs[0][:, lanes] = numer
    if not fused:
        previous = pltpu.roll(row, 1, 0) == row
        first = jnp.where(previous, 0.0, owner)
        outs[1][...] = dot(first, joint)
        outs[2][...] = denom


def attend(query, inv, deltas, cosine, sine, owner, mask, row, order, pages, fused):
    rows = query.shape[0]
    slots = owner.shape[0]
    heads = query.shape[1] // HD
    width = query.shape[1]
    if fused:
        out_shape = (jax.ShapeDtypeStruct((rows, width), bf16),)
    else:
        small = jax.ShapeDtypeStruct((rows, LANES), f32)
        out_shape = (jax.ShapeDtypeStruct((rows, width), f32), small, small)
    first = pl.BlockSpec((1, rows, width), lambda i: (0, 0, 0))

    def whole(value):
        return pl.BlockSpec(value.shape, lambda i, n=value.ndim: (0,) * n)

    steps = slots // SLOTS
    scratch = pltpu.VMEM((steps, heads * SLOTS, LANES), f32)
    fixed = (cosine, sine, owner, mask, row, pages)
    return pl.pallas_call(
        functools.partial(attention_kernel, heads, len(deltas), fused),
        grid=(1,),
        out_shape=out_shape,
        in_specs=[SMEM, whole(query), whole(inv)]
        + [first] * len(deltas)
        + [whole(value) for value in fixed],
        out_specs=tuple(pl.BlockSpec(s.shape, lambda i: (0, 0)) for s in out_shape),
        scratch_shapes=[scratch] * 4,
        compiler_params=params(),
        cost_estimate=cost(4e8, 8e6),
        name="attend",
    )(order, query, inv, *deltas, *fixed)


def down_kernel(offset, places, stored, aid_ref, *refs):
    inputs, (store_ref, out_ref, y_scr) = refs[: len(places)], refs[len(places) :]
    members = sum(len(group) for group in places)
    rows = inputs[0].shape[1]
    blocks = [None] * members
    for ref, group in zip(inputs, places):
        for i, j in enumerate(group):
            blocks[j] = (ref, i)
    for j in range(members):
        ref, i = blocks[j]
        for a in range(0, stored, 2):
            pair = jnp.concatenate([store_ref[a], store_ref[a + 1]], axis=1)
            result = jnp.dot(ref[i], pair, preferred_element_type=f32)
            y_scr[a, j * rows : (j + 1) * rows, :] = result[:, :LANES]
            y_scr[a + 1, j * rows : (j + 1) * rows, :] = result[:, LANES:]
    half = LANES // 2
    left = lax.broadcasted_iota(jnp.int32, (SEG, LANES), 1) < half
    seg_count = rows // SEG

    def pick(j, k):
        index = aid_ref[j * seg_count + k]
        value = y_scr[jnp.maximum(index, 0), pl.ds(j * rows + k * SEG, SEG), :]
        return jnp.where(index >= 0, value, 0.0)

    for j in range(0, members, 2):
        for k in range(seg_count):
            even, odd = pick(j, k), pick(j + 1, k)
            if offset:
                even = pltpu.roll(even, half, 1)
            else:
                odd = pltpu.roll(odd, half, 1)
            out_ref[pl.ds((j // 2) * rows + k * SEG, SEG), :] = jnp.where(
                left, even, odd
            ).astype(bf16)


def project_down(aid, arrays, store, offset):
    stored, width, _ = store.shape
    rows = arrays[0][0].shape[1]
    members = sum(value.shape[0] for value, _ in arrays)
    return pl.pallas_call(
        functools.partial(down_kernel, offset, [places for _, places in arrays], stored),
        grid=(1,),
        out_shape=jax.ShapeDtypeStruct((members // 2 * rows, LANES), bf16),
        in_specs=[SMEM]
        + [pl.BlockSpec(value.shape, lambda i: (0, 0, 0)) for value, _ in arrays]
        + [pl.BlockSpec((stored, width, LANES), lambda i: (0, 0, 0))],
        out_specs=pl.BlockSpec((members // 2 * rows, LANES), lambda i: (0, 0)),
        scratch_shapes=[pltpu.VMEM((stored, members * rows, LANES), f32)],
        compiler_params=params(),
        cost_estimate=cost(2 * members * rows * width * stored * LANES, 6e6),
        name="down",
    )(aid, *[value for value, _ in arrays], store)


def up_kernel(offset, members, stored, aid_ref, rank_ref, store_ref, keep_ref, send_ref, l_scr):
    rows = keep_ref.shape[1]
    half = LANES // 2
    seg_count = rows // SEG
    left = lax.broadcasted_iota(jnp.int32, (SEG, LANES), 1) < half
    for j in range(members):
        for k in range(seg_count):
            index = aid_ref[j * seg_count + k]
            value = rank_ref[pl.ds((j // 2) * rows + k * SEG, SEG), :].astype(f32)
            if (j % 2 == 1) != offset:
                value = pltpu.roll(value, half, 1)
            value = jnp.where(left != offset, value, 0.0)
            for a in range(stored):
                l_scr[pl.ds(j * rows + k * SEG, SEG), a * LANES : (a + 1) * LANES] = jnp.where(
                    index == a, value, 0.0
                ).astype(bf16)
    factors = jnp.concatenate([store_ref[a] for a in range(stored)], axis=1)
    for j in range(members):
        result = lax.dot_general(
            l_scr[j * rows : (j + 1) * rows, :], factors, NT, preferred_element_type=f32
        ).astype(bf16)
        (send_ref if j % 2 else keep_ref)[j // 2] = result


def project_up(aid, rank, store, members, rows, offset):
    stored, width, _ = store.shape
    half = jax.ShapeDtypeStruct((members // 2, rows, width), bf16)
    spec = pl.BlockSpec(half.shape, lambda i: (0, 0, 0))
    return pl.pallas_call(
        functools.partial(up_kernel, offset, members, stored),
        grid=(1,),
        out_shape=(half, half),
        in_specs=[
            SMEM,
            pl.BlockSpec(rank.shape, lambda i: (0, 0)),
            pl.BlockSpec((stored, width, LANES), lambda i: (0, 0, 1)),
        ],
        out_specs=(spec, spec),
        scratch_shapes=[pltpu.VMEM((members * rows, stored * LANES), bf16)],
        compiler_params=params(),
        cost_estimate=cost(2 * members * rows * width * stored * LANES, 6e6),
        name="up",
    )(aid, rank, store)


def block_dot_kernel(columns_ref, rows_ref, weight_ref, out_ref):
    out_ref[0] = jnp.dot(rows_ref[...], weight_ref[...], preferred_element_type=f32).astype(bf16)


def block_dot(columns, rows, weight, width):
    count = columns.shape[0]
    return pl.pallas_call(
        block_dot_kernel,
        grid_spec=pltpu.PrefetchScalarGridSpec(
            num_scalar_prefetch=1,
            grid=(count,),
            in_specs=[
                pl.BlockSpec(rows.shape, lambda i, table: (0, 0)),
                pl.BlockSpec((weight.shape[0], width), lambda i, table: (0, table[i])),
            ],
            out_specs=pl.BlockSpec((1, rows.shape[0], width), lambda i, table: (i, 0, 0)),
        ),
        out_shape=jax.ShapeDtypeStruct((count, rows.shape[0], width), bf16),
        compiler_params=params(),
        cost_estimate=cost(
            2 * count * rows.size * width, count * width * (weight.shape[0] + rows.shape[0]) * 2
        ),
        name="block_dot",
    )(columns, rows, weight)


def assemble_kernel(layout, columns_ref, *refs):
    inputs, (out_ref, sem) = refs[: len(layout)], refs[len(layout) :]
    copies = []
    for ref, (first, count) in zip(inputs, layout):
        width = ref.shape[2]
        for i in range(count):
            column = pl.multiple_of(columns_ref[first + i], LANES)
            copies.append(
                pltpu.make_async_copy(
                    ref.at[i], out_ref.at[:, pl.ds(column, width)], sem.at[first + i]
                )
            )
    for copy in copies:
        copy.start()
    for copy in copies:
        copy.wait()


def assemble(columns, arrays, full):
    rows = arrays[0].shape[1]
    layout, first = [], 0
    for value in arrays:
        layout.append((first, value.shape[0]))
        first += value.shape[0]
    return pl.pallas_call(
        functools.partial(assemble_kernel, layout),
        out_shape=jax.ShapeDtypeStruct((rows, full), bf16),
        in_specs=[SMEM] + [VMEM] * len(arrays),
        out_specs=pl.BlockSpec(memory_space=pl.ANY),
        scratch_shapes=[pltpu.SemaphoreType.DMA((first,))],
        compiler_params=params(),
        cost_estimate=cost(0, 4 * rows * full),
        name="assemble",
    )(columns, *arrays)


def gather_rows(own, axis, size):
    arrays = [(own[None], [0])]
    for bit in reversed(range(size.bit_length() - 1)):
        arrays = arrays + [
            (flip(value, axis, 1 << bit), [j ^ (1 << bit) for j in places])
            for value, places in arrays
        ]
    return arrays


def return_rows(keep, send, axis, size):
    addends = []
    for bit in range(size.bit_length() - 1):
        received = flip(send, axis, 1 << bit)
        addends = addends + [received] if bit else [keep, received]
        if keep.shape[0] == 1:
            break
        total = functools.reduce(jnp.add, [value.astype(f32) for value in addends]).astype(bf16)
        send = total[1::2]
        addends = [value[0::2] for value in addends]
        keep = addends[0]
    return addends


def body(
    hidden,
    norm_gain,
    query_matrix,
    output_weight,
    kv_pages,
    page_order,
    page_counts,
    page_trims,
    adapter_store,
    store_route,
    store_slot,
):
    tensor_size = lax.axis_size("tensor")
    group_size = lax.axis_size("group")
    tensor_index = lax.axis_index("tensor")
    group_index = lax.axis_index("group")
    rows, model = hidden.shape
    width = query_matrix.shape[1]
    heads_dev = width // HD
    split_count = tensor_size // KVH
    part_index = tensor_index % split_count
    slots = kv_pages.shape[0]
    half_size = kv_pages.shape[2]
    seg_count = rows // SEG

    hidden_wide = hidden.astype(f32)
    gain = norm_gain.astype(f32)
    own_hidden = lax.dynamic_slice_in_dim(hidden, tensor_index * width, width, 1).astype(f32)
    own_gain = lax.dynamic_slice_in_dim(gain, tensor_index * width, width, 0)
    own_rows = (own_hidden * own_gain[None, :]).astype(bf16)
    row_blocks = gather_rows(own_rows, "group", group_size)

    members = jnp.arange(group_size) ^ group_index
    routes = store_route[:, 0].reshape(group_size, seg_count)[members]
    slot_of = store_slot.reshape(group_size, seg_count)[members]
    aid = jnp.where(routes == group_index, slot_of, -1).reshape(-1).astype(jnp.int32)

    inv = lax.rsqrt(jnp.mean(hidden_wide * hidden_wide, axis=1, keepdims=True) + norm_eps)
    scaled = (hidden_wide * gain[None, :]).astype(bf16)
    query = jnp.dot(scaled, query_matrix, preferred_element_type=f32)

    lengths = page_counts[0] * (split_count * half_size) - page_trims[0]
    cosine, sine = tables((lengths - 1).astype(f32))
    trims = page_trims * jnp.where(part_index == split_count - 1, 1, 0)
    owner, mask, row = prepare(page_counts, trims, slots, half_size)

    bits = tensor_size.bit_length() - 1
    steps = [1 << k for k in range(bits - 1)] + [3 << (bits - 2)]

    def adapter(blocks, offset):
        rank = project_down(aid, blocks, adapter_store, offset)
        for step in steps:
            rank = (rank.astype(f32) + flip(rank, "tensor", step).astype(f32)).astype(bf16)
        keep, send = project_up(aid, rank, adapter_store, group_size, rows, offset)
        return return_rows(keep, send, "group", group_size)

    deltas = adapter(row_blocks, False)
    attention = functools.partial(
        attend,
        cosine=cosine,
        sine=sine,
        owner=owner,
        mask=mask,
        row=row,
        order=page_order,
        pages=kv_pages,
    )
    if split_count == 1:
        (attended,) = attention(query, inv, deltas, fused=True)
    else:
        delta = functools.reduce(jnp.add, [value[0].astype(f32) for value in deltas])
        wide = ((query + adapter_scale * delta) * inv).reshape(rows, heads_dev, HD)
        wide = wide * cosine[:, None] + jnp.roll(wide, HD // 2, 2) * sine[:, None]
        queries = wide.astype(bf16)
        levels = split_count.bit_length() - 1
        for level in range(levels):
            partner = flip(queries, "tensor", 1 << level)
            upper = part_index // 2**level % 2
            queries = jnp.where(
                upper == 0,
                jnp.concatenate([queries, partner], axis=1),
                jnp.concatenate([partner, queries], axis=1),
            )
        heads = heads_dev * split_count
        numer, top, total = attention(
            queries.reshape(rows, heads * HD).astype(f32), inv, [], fused=False
        )
        numer = numer.reshape(rows, heads, HD)
        top, total = top[:, :heads], total[:, :heads]
        for level in range(levels):
            other, other_top, other_total = flip((numer, top, total), "tensor", 1 << level)
            joint = jnp.maximum(top, other_top)
            own_scale, other_scale = jnp.exp(top - joint), jnp.exp(other_top - joint)
            numer = numer * own_scale[..., None] + other * other_scale[..., None]
            total = total * own_scale + other_total * other_scale
            top = joint
        attended = (
            lax.dynamic_slice_in_dim(
                numer / total[..., None], part_index * heads_dev, heads_dev, 1
            )
            .reshape(rows, width)
            .astype(bf16)
        )

    part_count = 2
    part_width = width // part_count
    orders = [[(p + i) % bits for i in range(bits)] for p in range(part_count)]

    def relative(order, first):
        found = []
        for n in range(1 << (bits - 1)):
            offset = steps[order[0]] if first else 0
            for i, k in enumerate(order[1:]):
                if n >> (bits - 2 - i) & 1:
                    offset ^= steps[k]
            found.append(offset)
        return found

    def columns_of(offsets, p):
        return ((jnp.array(offsets, jnp.int32) ^ tensor_index) * part_count + p).astype(jnp.int32)

    def partial(p, first):
        return block_dot(
            columns_of(relative(orders[p], first), p), attended, output_weight, part_width
        )

    row_blocks = gather_rows(attended, "group", group_size)
    sends = [partial(p, True) for p in range(part_count)]
    moving = [flip(sends[p], "tensor", steps[orders[p][0]]) for p in range(part_count)]
    keeps = [partial(p, False) for p in range(part_count)]
    deltas = adapter(row_blocks, True)
    own_delta = functools.reduce(jnp.add, [value[0].astype(f32) for value in deltas])
    finished = []
    for p in range(part_count):
        addends = [keeps[p], moving[p]]
        for k in orders[p][1:]:
            half = addends[0].shape[0] // 2
            send = functools.reduce(jnp.add, [v[half:].astype(f32) for v in addends]).astype(bf16)
            addends = [v[:half] for v in addends] + [flip(send, "tensor", steps[k])]
        total = functools.reduce(jnp.add, [v[0].astype(f32) for v in addends])
        lanes = slice(p * part_width, (p + 1) * part_width)
        total = total + own_hidden[:, lanes] + adapter_scale * own_delta[:, lanes]
        finished.append(total.astype(bf16)[None])

    arrays, table = [], []
    for p in range(part_count):
        value, offsets = finished[p], [0]
        for k in reversed(orders[p]):
            received = flip(value, "tensor", steps[k])
            other = [j ^ steps[k] for j in offsets]
            if len(offsets) * 2 == tensor_size:
                arrays += [value, received]
                table += [(j, p) for j in offsets + other]
            else:
                value = jnp.concatenate([value, received], axis=0)
                offsets = offsets + other
    offsets = jnp.array([j for j, _ in table], jnp.int32) ^ tensor_index
    columns = offsets * width + jnp.array([p * part_width for _, p in table], jnp.int32)
    return assemble(columns.astype(jnp.int32), arrays, model)


def solution(mesh):
    in_specs = (
        P("group", None),
        P(),
        P(None, "tensor"),
        P("tensor", None),
        P("group", "tensor", None, None),
        P("group", None),
        P("group", None),
        P("group", None),
        P("group", "tensor", None),
        P(),
        P(),
    )
    out_specs = P("group", None)
    return jax.shard_map(body, mesh=mesh, in_specs=in_specs, out_specs=out_specs, check_vma=False)
```

```python
import functools
import math

import jax
import jax.numpy as jnp
from jax import lax
from jax.experimental import pallas as pl
from jax.experimental.pallas import tpu as pltpu
from jax.sharding import PartitionSpec as P


KVH = 8
HD = 128
SEG = 16
PAGES_MAX = 8
LANES = 128
SLOTS = 8

adapter_scale = 2.0
norm_eps = 1e-05
rope_base = 500000.0
hidden_mask = -1e30

f32 = jnp.float32
bf16 = jnp.bfloat16
VMEM = pl.BlockSpec(memory_space=pltpu.VMEM)
SMEM = pl.BlockSpec(memory_space=pltpu.SMEM)
ANY = pl.BlockSpec(memory_space=pl.ANY)
NT = (((1,), (1,)), ((), ()))
TN = (((0,), (0,)), ((), ()))


def cost(flops, traffic):
    return pl.CostEstimate(flops=int(flops), bytes_accessed=int(traffic), transcendentals=0)


def params(mib):
    return pltpu.CompilerParams(vmem_limit_bytes=mib << 20)


def flip(value, axis, bits):
    return lax.ppermute(value, axis, [(i, i ^ bits) for i in range(lax.axis_size(axis))])


def tables(positions):
    half = HD // 2
    frequency = rope_base ** (-(jnp.arange(half).astype(f32) * 2.0) / HD)
    angles = positions[:, None] * frequency[None, :]
    cosine, sine = jnp.cos(angles), jnp.sin(angles)
    return jnp.concatenate([cosine, cosine], 1), jnp.concatenate([-sine, sine], 1)


def prep_kernel(half_size, counts_ref, trims_ref, owner_ref, mask_ref, row_ref):
    slots, rows = owner_ref.shape
    counts = counts_ref[...].astype(f32)
    trims = trims_ref[...].astype(f32)
    before = lax.broadcasted_iota(jnp.int32, (rows, rows), 0)
    after = lax.broadcasted_iota(jnp.int32, (rows, rows), 1)
    earlier = jnp.where(before < after, 1.0, 0.0).astype(bf16)
    start = jnp.dot(
        jnp.broadcast_to(counts, (8, rows)).astype(bf16), earlier, preferred_element_type=f32
    )[0:1]
    end = start + counts
    slot = lax.broadcasted_iota(jnp.int32, (slots, rows), 0).astype(f32)
    owner = jnp.where((slot >= start) & (slot < end), 1.0, 0.0)
    owner_ref[...] = owner
    last = jnp.where(slot == end - 1.0, trims, 0.0)
    used = half_size - jnp.sum(last, axis=1, keepdims=True)
    row = lax.broadcasted_iota(jnp.int32, (slots, rows), 1).astype(f32)
    row_ref[...] = jnp.broadcast_to(
        jnp.sum(owner * row, axis=1, keepdims=True), row_ref.shape
    )
    shape = mask_ref.shape
    place = lax.broadcasted_iota(jnp.int32, shape, 0) % SLOTS
    column = lax.broadcasted_iota(jnp.int32, shape, 1)
    fits = (column // half_size == place) & ((column % half_size).astype(f32) < used)
    mask_ref[...] = jnp.where(fits, 0.0, hidden_mask)


def prepare(counts, trims, slots, half_size):
    rows = counts.shape[1]
    return pl.pallas_call(
        functools.partial(prep_kernel, half_size),
        out_shape=(
            jax.ShapeDtypeStruct((slots, rows), f32),
            jax.ShapeDtypeStruct((slots, SLOTS * half_size), f32),
            jax.ShapeDtypeStruct((slots, LANES), f32),
        ),
        in_specs=[VMEM, VMEM],
        out_specs=(VMEM, VMEM, VMEM),
        compiler_params=params(4),
        cost_estimate=cost(1e6, 5e5),
        name="prep",
    )(counts, trims)


def attention_kernel(
    heads, extra, fused, order_ref, query_ref, inv_ref, *refs
):
    deltas, refs = refs[:extra], refs[extra:]
    cos_ref, sin_ref, owner_ref, mask_ref, row_ref, kv_ref = refs[:6]
    outs = refs[6:-4]
    q_scr, o_scr, m_scr, l_scr = refs[-4:]
    slots = owner_ref.shape[0]
    steps = slots // SLOTS
    half_size = kv_ref.shape[2]
    owner = owner_ref[...]
    owner_low = owner.astype(bf16)
    for head in range(heads):
        lanes = slice(head * HD, (head + 1) * HD)
        value = query_ref[:, lanes]
        if fused:
            for ref in deltas:
                value = value + adapter_scale * ref[0, :, lanes].astype(f32)
            value = value * inv_ref[...]
            value = value * cos_ref[...] + pltpu.roll(value, HD // 2, 1) * sin_ref[...]
        spread = jnp.dot(owner_low, value.astype(bf16), preferred_element_type=f32)
        q_scr[:, head * SLOTS : (head + 1) * SLOTS, :] = spread.reshape(steps, SLOTS, HD)

    def step(b, carry):
        pages = [kv_ref[order_ref[0, b * SLOTS + i], 0] for i in range(SLOTS)]
        keys = jnp.concatenate([page[:, :HD] for page in pages], axis=0)
        values = jnp.concatenate([page[:, HD:] for page in pages], axis=0)
        scores = lax.dot_general(
            q_scr[b].astype(bf16), keys, NT, preferred_element_type=f32
        ) * (1.0 / math.sqrt(HD))
        width = SLOTS * half_size
        mask = mask_ref[pl.ds(pl.multiple_of(b * SLOTS, SLOTS), SLOTS), :]
        scores = (scores.reshape(heads, SLOTS, width) + mask[None]).reshape(heads * SLOTS, width)
        top = jnp.max(scores, axis=1, keepdims=True)
        weights = jnp.exp(scores - top).astype(bf16)
        total = jnp.sum(weights.astype(f32), axis=1, keepdims=True)
        o_scr[b] = jnp.dot(weights, values, preferred_element_type=f32)
        m_scr[b] = jnp.broadcast_to(top, (heads * SLOTS, LANES))
        l_scr[b] = jnp.broadcast_to(total, (heads * SLOTS, LANES))
        return carry

    lax.fori_loop(0, steps, step, 0, unroll=4 if steps % 4 == 0 else 1)

    lane = lax.broadcasted_iota(jnp.int32, (slots, LANES), 1)
    tops = jnp.zeros((slots, LANES), f32)
    totals = jnp.zeros((slots, LANES), f32)
    for head in range(heads):
        part = slice(head * SLOTS, (head + 1) * SLOTS)
        tops = jnp.where(lane == head, m_scr[:, part, :].reshape(slots, LANES), tops)
        totals = jnp.where(lane == head, l_scr[:, part, :].reshape(slots, LANES), totals)
    row = row_ref[...]
    joint = tops
    distance = 1
    while distance < PAGES_MAX:
        for shift in (distance, slots - distance):
            same = pltpu.roll(row, shift, 0) == row
            joint = jnp.where(same, jnp.maximum(joint, pltpu.roll(joint, shift, 0)), joint)
        distance *= 2
    factor = jnp.exp(tops - joint)
    dot = functools.partial(
        lax.dot_general,
        dimension_numbers=TN,
        precision=lax.Precision.HIGHEST,
        preferred_element_type=f32,
    )
    denom = dot(owner, totals * factor)
    for head in range(heads):
        part = slice(head * SLOTS, (head + 1) * SLOTS)
        lanes = slice(head * HD, (head + 1) * HD)
        value = o_scr[:, part, :].reshape(slots, HD) * factor[:, head : head + 1]
        numer = dot(owner, value)
        if fused:
            outs[0][:, lanes] = (numer / denom[:, head : head + 1]).astype(bf16)
        else:
            outs[0][:, lanes] = numer
    if not fused:
        previous = pltpu.roll(row, 1, 0) == row
        first = jnp.where(previous, 0.0, owner)
        outs[1][...] = dot(first, joint)
        outs[2][...] = denom


def attend(query, inv, deltas, cosine, sine, owner, mask, row, order, pages, fused):
    rows = query.shape[0]
    slots = owner.shape[0]
    heads = query.shape[1] // HD
    width = query.shape[1]
    if fused:
        out_shape = (jax.ShapeDtypeStruct((rows, width), bf16),)
    else:
        small = jax.ShapeDtypeStruct((rows, LANES), f32)
        out_shape = (jax.ShapeDtypeStruct((rows, width), f32), small, small)
    first = pl.BlockSpec((1, rows, width), lambda i: (0, 0, 0))

    def whole(value):
        return pl.BlockSpec(value.shape, lambda i, n=value.ndim: (0,) * n)

    steps = slots // SLOTS
    scratch = pltpu.VMEM((steps, heads * SLOTS, LANES), f32)
    fixed = (cosine, sine, owner, mask, row, pages)
    return pl.pallas_call(
        functools.partial(attention_kernel, heads, len(deltas), fused),
        grid=(1,),
        out_shape=out_shape,
        in_specs=[SMEM, whole(query), whole(inv)]
        + [first] * len(deltas)
        + [whole(value) for value in fixed],
        out_specs=tuple(pl.BlockSpec(s.shape, lambda i: (0, 0)) for s in out_shape),
        scratch_shapes=[scratch] * 4,
        compiler_params=params(24),
        cost_estimate=cost(4e8, 8e6),
        name="attend",
    )(order, query, inv, *deltas, *fixed)


def capacity_of(members, seg_count):
    return max(2, (2 * seg_count + members - 1) // members)


def own_kernel(hidden_ref, gain_ref, out_ref, rows_scr, gain_scr, sem):
    width = out_ref.shape[2]
    start = pl.multiple_of(lax.axis_index("tensor") * width, LANES)
    rows = pltpu.make_async_copy(hidden_ref.at[:, pl.ds(start, width)], rows_scr, sem.at[0])
    gain = pltpu.make_async_copy(gain_ref.at[:, pl.ds(start, width)], gain_scr, sem.at[1])
    rows.start()
    gain.start()
    rows.wait()
    gain.wait()
    out_ref[0] = (rows_scr[...].astype(f32) * gain_scr[...].astype(f32)).astype(bf16)


def scale_own(hidden, gain, width):
    rows = hidden.shape[0]
    return pl.pallas_call(
        own_kernel,
        out_shape=jax.ShapeDtypeStruct((1, rows, width), bf16),
        in_specs=[ANY, ANY],
        out_specs=VMEM,
        scratch_shapes=[
            pltpu.VMEM((rows, width), bf16),
            pltpu.VMEM((1, width), bf16),
            pltpu.SemaphoreType.DMA((2,)),
        ],
        compiler_params=params(8),
        cost_estimate=cost(rows * width, 4 * rows * width),
        name="own",
    )(hidden, gain)


def query_kernel(hidden_ref, gain_ref, weight_ref, store_ref, out_ref, inv_ref, kept_ref, *scr):
    h_scr, w_scr, sem, store_sem = scr
    chunks = h_scr.shape[0]
    depth = h_scr.shape[2]
    copies = []
    for i in range(chunks):
        span = pl.ds(i * depth, depth)
        copies.append(
            (
                pltpu.make_async_copy(hidden_ref.at[:, span], h_scr.at[i], sem.at[2 * i]),
                pltpu.make_async_copy(weight_ref.at[span], w_scr.at[i], sem.at[2 * i + 1]),
            )
        )
    for pair in copies:
        for copy in pair:
            copy.start()
    stores = [
        pltpu.make_async_copy(store_ref.at[a], kept_ref.at[a], store_sem.at[a])
        for a in range(store_ref.shape[0])
    ]
    for copy in stores:
        copy.start()
    squares = None
    for i, pair in enumerate(copies):
        for copy in pair:
            copy.wait()
        wide = h_scr[i].astype(f32)
        power = jnp.sum(wide * wide, axis=1, keepdims=True)
        squares = power if i == 0 else squares + power
        scaled = (wide * gain_ref[:, i * depth : (i + 1) * depth].astype(f32)).astype(bf16)
        product = jnp.dot(scaled, w_scr[i], preferred_element_type=f32)
        if i == 0:
            out_ref[...] = product
        else:
            out_ref[...] += product
    inv_ref[...] = lax.rsqrt(squares / (chunks * depth) + norm_eps)
    for copy in stores:
        copy.wait()


def project_query(hidden, gain, weight, store):
    rows, model = hidden.shape
    width = weight.shape[1]
    chunks = 8
    depth = model // chunks
    return pl.pallas_call(
        query_kernel,
        out_shape=(
            pltpu.VMEM((rows, width), f32),
            pltpu.VMEM((rows, 1), f32),
            pltpu.VMEM(store.shape, bf16),
        ),
        in_specs=[ANY, VMEM, ANY, ANY],
        out_specs=(VMEM, VMEM, VMEM),
        scratch_shapes=[
            pltpu.VMEM((chunks, rows, depth), bf16),
            pltpu.VMEM((chunks, depth, width), bf16),
            pltpu.SemaphoreType.DMA((2 * chunks,)),
            pltpu.SemaphoreType.DMA((store.shape[0],)),
        ],
        compiler_params=params(32),
        cost_estimate=cost(2 * rows * weight.size, 2 * (weight.size + store.size + hidden.size)),
        name="query",
    )(hidden, gain, weight, store)


def fetch_kernel(first, weight_ref, kept_ref, sem):
    copies = []
    pieces = sem.shape[0]
    depth = kept_ref.shape[0] // pieces
    for i in range(pieces):
        copies.append(
            pltpu.make_async_copy(
                weight_ref.at[pl.ds(first + i * depth, depth)],
                kept_ref.at[pl.ds(i * depth, depth)],
                sem.at[i],
            )
        )
    for copy in copies:
        copy.start()
    for copy in copies:
        copy.wait()


def fetch(weight, first, depth):
    return pl.pallas_call(
        functools.partial(fetch_kernel, first),
        out_shape=pltpu.VMEM((depth, weight.shape[1]), bf16),
        in_specs=[ANY],
        out_specs=VMEM,
        scratch_shapes=[pltpu.SemaphoreType.DMA((4,))],
        compiler_params=params(1),
        cost_estimate=cost(0, 2 * depth * weight.shape[1]),
        name="fetch",
    )(weight)


def block_kernel(offsets, addends, parts, rows_ref, *refs):
    weights, refs = refs[:parts], refs[parts:]
    added, outs = refs[:addends], refs[addends:]
    width = outs[0].shape[1]
    depth = rows_ref.shape[1] // parts
    index = lax.axis_index("tensor")
    for i, offset in enumerate(offsets):
        start = pl.multiple_of((index ^ offset) * width, LANES)
        total = None
        for p, weight_ref in enumerate(weights):
            product = jnp.dot(
                rows_ref[:, p * depth : (p + 1) * depth],
                weight_ref[:, pl.ds(start, width)],
                preferred_element_type=f32,
            )
            total = product if p == 0 else total + product
        if i == 0:
            for ref in added:
                total = total + ref[...].astype(f32)
        outs[i][...] = total.astype(bf16)


def block_dot(offsets, rows, weights, added=()):
    width = rows.shape[1]
    out = jax.ShapeDtypeStruct((rows.shape[0], width), bf16)
    count = len(offsets)
    return pl.pallas_call(
        functools.partial(block_kernel, offsets, len(added), len(weights)),
        out_shape=(out,) * count,
        in_specs=[VMEM] * (1 + len(weights) + len(added)),
        out_specs=(VMEM,) * count,
        compiler_params=params(8),
        cost_estimate=cost(2 * count * rows.size * width, 4 * count * rows.size),
        name="block_dot",
    )(rows, *weights, *added)


def finish_kernel(sums, deltas, parts, rows_ref, *refs):
    weights, refs = refs[:parts], refs[parts:]
    added, refs = refs[:sums], refs[sums:]
    returned, (hidden_ref, out_ref, h_scr, sem) = refs[:deltas], refs[deltas:]
    width = out_ref.shape[1]
    depth = rows_ref.shape[1] // parts
    start = pl.multiple_of(lax.axis_index("tensor") * width, LANES)
    copy = pltpu.make_async_copy(hidden_ref.at[:, pl.ds(start, width)], h_scr, sem)
    copy.start()
    total = None
    for p, weight_ref in enumerate(weights):
        product = jnp.dot(
            rows_ref[:, p * depth : (p + 1) * depth],
            weight_ref[:, pl.ds(start, width)],
            preferred_element_type=f32,
        )
        total = product if p == 0 else total + product
    for ref in added:
        total = total + ref[...].astype(f32)
    delta = returned[0][0].astype(f32)
    for ref in returned[1:]:
        delta = delta + ref[0].astype(f32)
    copy.wait()
    out_ref[...] = (h_scr[...].astype(f32) + (total + adapter_scale * delta)).astype(bf16)


def finish(rows, weights, added, deltas, hidden):
    width = rows.shape[1]
    return pl.pallas_call(
        functools.partial(finish_kernel, len(added), len(deltas), len(weights)),
        out_shape=jax.ShapeDtypeStruct(rows.shape, bf16),
        in_specs=[VMEM] * (1 + len(weights) + len(added) + len(deltas)) + [ANY],
        out_specs=VMEM,
        scratch_shapes=[pltpu.VMEM(rows.shape, bf16), pltpu.SemaphoreType.DMA],
        compiler_params=params(8),
        cost_estimate=cost(2 * rows.size * width, 8 * rows.size),
        name="finish",
    )(rows, *weights, *added, *deltas, hidden)


def served(route_ref, slot_ref, members, seg_count, capacity):
    group = lax.axis_index("group")
    table = []
    for j in range(members):
        base = (group ^ j) * seg_count
        count = jnp.int32(0)
        for k in range(seg_count):
            here = route_ref[base + k] == group
            index = jnp.where(here, slot_ref[base + k], -1)
            place = jnp.where(here, jnp.minimum(count, capacity - 1), capacity)
            table.append((index, place))
            count = count + here.astype(jnp.int32)
    return table


def down_kernel(offset, places, capacity, route_ref, slot_ref, *refs):
    inputs, (store_ref, out_ref, y_scr, c_scr) = refs[: len(places)], refs[len(places) :]
    stored = store_ref.shape[0]
    members = sum(len(group) for group in places)
    rows = inputs[0].shape[1]
    seg_count = rows // SEG
    half = LANES // 2
    c_scr[...] = jnp.zeros_like(c_scr)
    for ref, group in zip(inputs, places):
        for i, j in enumerate(group):
            for a in range(0, stored, 2):
                pair = jnp.concatenate(
                    [store_ref[a, :, :LANES], store_ref[a + 1, :, :LANES]], axis=1
                )
                result = jnp.dot(ref[i], pair, preferred_element_type=f32)
                y_scr[a, j * rows : (j + 1) * rows, :] = result[:, :LANES]
                y_scr[a + 1, j * rows : (j + 1) * rows, :] = result[:, LANES:]
    table = served(route_ref, slot_ref, members, seg_count, capacity)
    for j in range(members):
        for k in range(seg_count):
            index, place = table[j * seg_count + k]
            c_scr[j, pl.ds(pl.multiple_of(place * SEG, SEG), SEG), :] = y_scr[
                jnp.maximum(index, 0), pl.ds(j * rows + k * SEG, SEG), :
            ]
    used = capacity * SEG
    left = lax.broadcasted_iota(jnp.int32, (used, LANES), 1) < half
    for j in range(0, members, 2):
        even, odd = c_scr[j, :used], c_scr[j + 1, :used]
        if offset:
            even = pltpu.roll(even, half, 1)
        else:
            odd = pltpu.roll(odd, half, 1)
        out_ref[(j // 2) * used : (j // 2 + 1) * used, :] = jnp.where(left, even, odd).astype(bf16)


def project_down(route, slot, arrays, store, offset):
    stored, width, _ = store.shape
    rows = arrays[0][0].shape[1]
    members = sum(value.shape[0] for value, _ in arrays)
    capacity = capacity_of(members, rows // SEG)
    return pl.pallas_call(
        functools.partial(down_kernel, offset, [places for _, places in arrays], capacity),
        out_shape=jax.ShapeDtypeStruct((members // 2 * capacity * SEG, LANES), bf16),
        in_specs=[SMEM, SMEM] + [VMEM] * (len(arrays) + 1),
        out_specs=VMEM,
        scratch_shapes=[
            pltpu.VMEM((stored, members * rows, LANES), f32),
            pltpu.VMEM((members, (capacity + 1) * SEG, LANES), f32),
        ],
        compiler_params=params(12),
        cost_estimate=cost(2 * members * rows * width * stored * LANES, 2e6),
        name="down",
    )(route, slot, *[value for value, _ in arrays], store)


def up_kernel(
    offset, members, capacity, route_ref, slot_ref, rank_ref, store_ref, keep_ref, send_ref, l_scr, y_scr
):
    stored = store_ref.shape[0]
    width = store_ref.shape[1]
    rows = keep_ref.shape[1]
    seg_count = rows // SEG
    half = LANES // 2
    used = capacity * SEG
    table = served(route_ref, slot_ref, members, seg_count, capacity)
    left = lax.broadcasted_iota(jnp.int32, (used, LANES), 1) < half
    l_scr[...] = jnp.zeros_like(l_scr)
    for j in range(members):
        value = rank_ref[(j // 2) * used : (j // 2 + 1) * used, :].astype(f32)
        if (j % 2 == 1) != offset:
            value = pltpu.roll(value, half, 1)
        value = jnp.where(left != offset, value, 0.0)
        y_scr[j * used : (j + 1) * used, :LANES] = value
    for j in range(members):
        for k in range(seg_count):
            index, place = table[j * seg_count + k]
            source = j * used + jnp.minimum(place, capacity - 1) * SEG
            value = y_scr[pl.ds(pl.multiple_of(source, SEG), SEG), :LANES]
            target = j * (used + SEG) + place * SEG
            l_scr[jnp.maximum(index, 0), pl.ds(pl.multiple_of(target, SEG), SEG), :] = value.astype(
                bf16
            )
    lhs = jnp.concatenate(
        [
            jnp.concatenate(
                [l_scr[a, j * (used + SEG) : j * (used + SEG) + used, :] for j in range(members)],
                axis=0,
            )
            for a in range(stored)
        ],
        axis=1,
    )
    piece = min(width, 2 * LANES)
    for n in range(0, width, piece):
        factors = jnp.concatenate(
            [store_ref[a, n : n + piece, LANES:] for a in range(stored)], axis=1
        )
        y_scr[:, n : n + piece] = lax.dot_general(lhs, factors, NT, preferred_element_type=f32)
    for j in range(members):
        out_ref = send_ref if j % 2 else keep_ref
        for k in range(seg_count):
            index, place = table[j * seg_count + k]
            source = j * used + jnp.minimum(place, capacity - 1) * SEG
            value = y_scr[pl.ds(pl.multiple_of(source, SEG), SEG), :]
            out_ref[j // 2, k * SEG : (k + 1) * SEG, :] = jnp.where(index >= 0, value, 0.0).astype(
                bf16
            )


def project_up(route, slot, rank, store, members, rows, offset):
    stored, width, _ = store.shape
    capacity = capacity_of(members, rows // SEG)
    half = jax.ShapeDtypeStruct((members // 2, rows, width), bf16)
    return pl.pallas_call(
        functools.partial(up_kernel, offset, members, capacity),
        out_shape=(half, half),
        in_specs=[SMEM, SMEM, VMEM, VMEM],
        out_specs=(VMEM, VMEM),
        scratch_shapes=[
            pltpu.VMEM((stored, members * (capacity + 1) * SEG, LANES), bf16),
            pltpu.VMEM((members * capacity * SEG, width), f32),
        ],
        compiler_params=params(12),
        cost_estimate=cost(members * rows * width * stored * LANES, 2e6),
        name="up",
    )(route, slot, rank, store)


def assemble_kernel(offsets, *refs):
    inputs, (out_ref, sem) = refs[: len(offsets)], refs[len(offsets) :]
    index = lax.axis_index("tensor")
    copies = []
    for i, (ref, offset) in enumerate(zip(inputs, offsets)):
        width = ref.shape[1]
        start = pl.multiple_of((index ^ offset) * width, LANES)
        copies.append(pltpu.make_async_copy(ref, out_ref.at[:, pl.ds(start, width)], sem.at[i]))
    for copy in copies:
        copy.start()
    for copy in copies:
        copy.wait()


def assemble(blocks):
    rows, width = blocks[0][0].shape
    count = len(blocks)
    return pl.pallas_call(
        functools.partial(assemble_kernel, [offset for _, offset in blocks]),
        out_shape=jax.ShapeDtypeStruct((rows, count * width), bf16),
        in_specs=[VMEM] * count,
        out_specs=ANY,
        scratch_shapes=[pltpu.SemaphoreType.DMA((count,))],
        compiler_params=params(1),
        cost_estimate=cost(0, 4 * rows * count * width),
        name="assemble",
    )(*[value for value, _ in blocks])


def gather_rows(own, axis, size):
    arrays = [(own, [0])]
    for bit in reversed(range(size.bit_length() - 1)):
        more = []
        for value, places in arrays:
            more.append((flip(value, axis, 1 << bit), [j ^ (1 << bit) for j in places]))
        arrays = arrays + more
    return arrays


def return_rows(keep, send, axis, size):
    addends = [keep]
    for bit in range(size.bit_length() - 1):
        addends.append(flip(send, axis, 1 << bit))
        if 2 << bit < size:
            take = [value[1::2] if value.shape[0] > 1 else value for value in addends]
            total = functools.reduce(jnp.add, [value.astype(f32) for value in take])
            send = total.astype(bf16)
            if 4 << bit < size:
                addends = [value[0::2] for value in addends]
    return addends


def reduce_scatter(attended, weights, bits, steps):
    if bits == 3:
        one, two, three = steps
        far, first, third = block_dot(
            [one ^ two ^ three, three ^ one, one ^ two], attended, weights
        )
        far = flip(far, "tensor", one)
        from_three = flip(first, "tensor", three)
        from_one = flip(third, "tensor", one)
        (second,) = block_dot([two ^ three], attended, weights, [far])
        from_two = flip(second, "tensor", two)
        sums = []
        for step, value in ((one, from_three), (two, from_one), (three, from_two)):
            (send,) = block_dot([step], attended, weights, [value])
            sums.append(flip(send, "tensor", step))
        return sums
    offsets, sums = [0], []
    for step in steps:
        offsets = offsets + [j ^ step for j in offsets]
    blocks = dict(zip(offsets, block_dot(offsets, attended, weights)))
    for n, step in enumerate(steps):
        rest = [0]
        for later in steps[n + 1 :]:
            rest = rest + [j ^ later for j in rest]
        send = jnp.stack([blocks[j ^ step] for j in rest])
        received = flip(send, "tensor", step)
        sums.append(received[0])
        for i, j in enumerate(rest[1:]):
            blocks[j] = (blocks[j].astype(f32) + received[i + 1].astype(f32)).astype(bf16)
    return sums


def all_gather(value, bits, steps):
    if bits == 3:
        one, two, three = steps
        at = {0: value}
        for step in steps:
            at[step] = flip(value, "tensor", step)
        for step, source in ((three, one), (one, two), (two, three)):
            at[step ^ source] = flip(at[source], "tensor", step)
        at[one ^ two ^ three] = flip(at[one ^ two], "tensor", three)
        return [(at[j], j) for j in at]
    blocks = [(value, 0)]
    for step in steps:
        received = flip(jnp.stack([value for value, _ in blocks]), "tensor", step)
        blocks = blocks + [(received[i], j ^ step) for i, (_, j) in enumerate(blocks)]
    return blocks


def body(
    hidden,
    norm_gain,
    query_matrix,
    output_weight,
    kv_pages,
    page_order,
    page_counts,
    page_trims,
    adapter_store,
    store_route,
    store_slot,
):
    tensor_size = lax.axis_size("tensor")
    group_size = lax.axis_size("group")
    tensor_index = lax.axis_index("tensor")
    rows, model = hidden.shape
    width = query_matrix.shape[1]
    heads_dev = width // HD
    split_count = tensor_size // KVH
    part_index = tensor_index % split_count
    slots = kv_pages.shape[0]
    half_size = kv_pages.shape[2]

    route = store_route.reshape(-1)
    gain = norm_gain.reshape(1, model)
    own_rows = scale_own(hidden, gain, width)
    row_blocks = gather_rows(own_rows, "group", group_size)
    query, inv, store = project_query(hidden, gain, query_matrix, adapter_store)

    weight_parts = 4
    depth = width // weight_parts
    weights = []
    for p in range(weight_parts):
        weights.append(fetch(output_weight, p * depth, depth))

    lengths = page_counts[0] * (split_count * half_size) - page_trims[0]
    cosine, sine = tables((lengths - 1).astype(f32))
    trims = page_trims * jnp.where(part_index == split_count - 1, 1, 0)
    owner, mask, row = prepare(page_counts, trims, slots, half_size)

    bits = tensor_size.bit_length() - 1
    steps = [1 << k for k in range(bits - 1)] + [3 << (bits - 2)]

    def adapter(blocks, offset):
        rank = project_down(route, store_slot, blocks, store, offset)
        for step in steps:
            received = flip(rank, "tensor", step)
            rank = (rank.astype(f32) + received.astype(f32)).astype(bf16)
        keep, send = project_up(route, store_slot, rank, store, group_size, rows, offset)
        return return_rows(keep, send, "group", group_size)

    deltas = adapter(row_blocks, False)
    attention = functools.partial(
        attend,
        cosine=cosine,
        sine=sine,
        owner=owner,
        mask=mask,
        row=row,
        order=page_order,
        pages=kv_pages,
    )
    if split_count == 1:
        (attended,) = attention(query, inv, deltas, fused=True)
    else:
        delta = functools.reduce(jnp.add, [value[0].astype(f32) for value in deltas])
        wide = ((query + adapter_scale * delta) * inv).reshape(rows, heads_dev, HD)
        wide = wide * cosine[:, None] + jnp.roll(wide, HD // 2, 2) * sine[:, None]
        queries = wide.astype(bf16)
        levels = split_count.bit_length() - 1
        for level in range(levels):
            partner = flip(queries, "tensor", 1 << level)
            upper = part_index // 2**level % 2
            queries = jnp.where(
                upper == 0,
                jnp.concatenate([queries, partner], axis=1),
                jnp.concatenate([partner, queries], axis=1),
            )
        heads = heads_dev * split_count
        numer, top, total = attention(
            queries.reshape(rows, heads * HD).astype(f32), inv, [], fused=False
        )
        numer = numer.reshape(rows, heads, HD)
        top, total = top[:, :heads], total[:, :heads]
        for level in range(levels):
            other, other_top, other_total = flip((numer, top, total), "tensor", 1 << level)
            joint = jnp.maximum(top, other_top)
            own_scale, other_scale = jnp.exp(top - joint), jnp.exp(other_top - joint)
            numer = numer * own_scale[..., None] + other * other_scale[..., None]
            total = total * own_scale + other_total * other_scale
            top = joint
        attended = (
            lax.dynamic_slice_in_dim(
                numer / total[..., None], part_index * heads_dev, heads_dev, 1
            )
            .reshape(rows, width)
            .astype(bf16)
        )

    row_blocks = gather_rows(attended[None], "group", group_size)
    sums = reduce_scatter(attended, weights, bits, steps)
    deltas = adapter(row_blocks, True)
    finished = finish(attended, weights, sums, deltas, hidden)
    return assemble(all_gather(finished, bits, steps))


def solution(mesh):
    in_specs = (
        P("group", None),
        P(),
        P(None, "tensor"),
        P("tensor", None),
        P("group", "tensor", None, None),
        P("group", None),
        P("group", None),
        P("group", None),
        P("group", "tensor", None),
        P(),
        P(),
    )
    out_specs = P("group", None)

    return jax.shard_map(body, mesh=mesh, in_specs=in_specs, out_specs=out_specs, check_vma=False)
```
